32 devices in a mesh: sys: 2 (over y), dom: 4 (over z), rank: 2 (over x), sub: 2 (over core).
Axes of the slice: x: 2, y: 2, z: 4, core: 2. Of those that a mesh axis runs over, the one named last changes fastest.
Arguments:
- positions: float32 [3, 8, 16, 4, 128], P(None, ('sys', 'dom'), ('rank', 'sub')), parts along dimension 1, may hold values from 0 to 1
- charges: float32 [8, 16, 4, 128], P(('sys', 'dom'), ('rank', 'sub')), parts along dimension 0, may hold values from -3 to 3
- neighbours: int32 [8, 16, 4, 8], P(('sys', 'dom'), ('rank', 'sub')), parts along dimension 0, may hold values from 0 to 26, all different within a row
Outputs:
- forces: float32 [3, 8, 16, 4, 128], P(None, ('sys', 'dom'), ('rank', 'sub')), parts along dimension 1
The draws below stay inside these ranges and needn't reach their ends.
There are 2 independent parts, one for each index of `sys`. The reference program is written for one: setup_inputs(seed, part) draws one part's arguments, and reference() takes and returns one part's arrays. A program takes and returns all parts, laid end to end along the dimension named above; each array names one. Nothing has to cross between parts.
Inputs may be any that keep to these rules, and one draw needn't show every extreme that they name: `neighbours`: entry s names the cell displaced by (s // 9 - 1, s // 3 % 3 - 1, s % 3 - 1) cells along z, y and x; the 8 entries of a cell are distinct.
All inputs are finite; a program needn't handle non-finite values.
Results may differ from the reference program's by a relative error of at most 0.0003.
Values sent between devices are 32-bit elements; how exact they have to be, the bound alone decides.
A program may use at most 128 MiB of HBM per device.

```python
import math
import jax
import jax.numpy as jnp
from jax import lax

GRID = 256
ATOMS = 128
K = 8
CX = 4
PZ = 64
BY = 16
BX = 64
NCZ = 4
NCY = 16


def levels(key, shape, cuts, low, high):
    gain = 1.0
    for position, shards_of in cuts:
        steps = jax.random.uniform(jax.random.fold_in(jax.random.fold_in(key, 6), position), (shards_of,), jnp.float32, low / len(cuts), high / len(cuts))
        gain = gain * jnp.repeat(jnp.exp(steps), shape[position] // shards_of).reshape((-1,) + (1,) * (len(shape) - 1 - position))
    return gain


def picks_of(rng, rows, count, top, lift):
    ranking = jax.random.permutation(jax.random.fold_in(rng, 1), count)
    favour = ranking
    for power in range(3):
        favour = favour * favour // count
    favour = favour * lift // count
    lots = jax.random.randint(jax.random.fold_in(rng, 2), (rows, count), 0, 4096) + favour
    sure = jax.random.permutation(jax.random.fold_in(rng, 3), rows)[jnp.arange(count) % rows]
    lots = jnp.where(jnp.arange(rows)[:, None] == sure[None, :], 1 << 14, lots)
    merit = lots * count + jnp.arange(count)
    return lax.top_k(merit.astype(jnp.int32), top)[1].astype(jnp.int32)


def normal_values(own_key, extent, width, limit, shards=(), kind=jnp.bfloat16):
    values = width * jax.random.normal(own_key, extent, jnp.float32)
    if shards:
        values = values * levels(own_key, extent, shards, -0.22, 0.18)
    return jnp.clip(values, -limit, limit).astype(kind)


def setup_inputs(seed: int = 0, part: int = 0) -> dict:
    key_list = jax.random.split(jax.random.key(seed), 4)
    part_splits = jax.random.split(jax.random.fold_in(key_list[3], part), 4)
    return {
        "positions": jnp.clip(1.0 * jax.random.uniform(part_splits[0], (3, NCZ, NCY, CX, ATOMS), jnp.float32) ** levels(part_splits[0], (3, NCZ, NCY, CX, ATOMS), ((1, 4), (2, 4)), -0.2, 0.2), 0.0, 1.0),
        "charges": normal_values(part_splits[1], (NCZ, NCY, CX, ATOMS), 0.5, 3.0, ((0, 4), (1, 4)), jnp.float32),
        "neighbours": picks_of(part_splits[2], NCZ * NCY * CX, 27, K, 0).reshape((NCZ, NCY, CX, K)),
    }


ewald_beta = 0.7
soften = 1.0
highest = lax.Precision.HIGHEST

def bspline(offsets):
    clipped = jnp.clip(offsets, 0.0, 4.0)
    lift_one = jnp.maximum(clipped - 1.0, 0.0)
    lift_two = jnp.maximum(clipped - 2.0, 0.0)
    lift_three = jnp.maximum(clipped - 3.0, 0.0)
    spline_value = (clipped ** 3 - 4.0 * lift_one ** 3 + 6.0 * lift_two ** 3 - 4.0 * lift_three ** 3) / 6.0
    spline_slope = (clipped ** 2 - 4.0 * lift_one ** 2 + 6.0 * lift_two ** 2 - 4.0 * lift_three ** 2) / 2.0
    return (spline_value, spline_slope)

def window_weights(coords, span):
    return bspline(coords[..., None] + 3.0 - jnp.arange(span, dtype=jnp.float32))

def periodic_weights(coords):
    offsets = coords[..., None] - jnp.arange(GRID, dtype=jnp.float32)
    offsets = jnp.where(offsets < 0.0, offsets + GRID, offsets)
    return bspline(offsets)

def pair_terms(own_cells, other_cells, offset):
    displace = own_cells[:3, :, :, None] - other_cells[:3, :, None, :] - offset[:, :, None, None]
    dist_square = lax.optimization_barrier(jnp.sum(displace * displace, axis=0)) + soften
    distance = jnp.sqrt(dist_square)
    scaled = ewald_beta * distance
    radial = (jax.scipy.special.erfc(scaled) / distance + 2.0 * ewald_beta / math.sqrt(math.pi) * jnp.exp(-scaled * scaled)) / dist_square
    weight = own_cells[3][:, :, None] * other_cells[3][:, None, :] * radial
    return lax.optimization_barrier(jnp.sum(weight[None] * displace, axis=3))

def spread_rows(atom_data, span_z, span_y, block_x):
    rows_z, rows_y, cells_x, atom_count = atom_data.shape[1:]
    corner_x = (jnp.arange(cells_x, dtype=jnp.float32) * block_x)[:, None]
    place_z = atom_data[0].reshape(rows_z, rows_y, cells_x * atom_count)
    place_y = atom_data[1].reshape(rows_z, rows_y, cells_x * atom_count)
    place_x = (atom_data[2] + corner_x).reshape(rows_z, rows_y, cells_x * atom_count)
    charge_rows = atom_data[3].reshape(rows_z, rows_y, cells_x * atom_count)
    weight_z = window_weights(place_z, span_z)[0]
    weight_y = window_weights(place_y, span_y)[0]
    weight_x = periodic_weights(place_x)[0]
    weighted = charge_rows[..., None, None] * weight_z[..., :, None] * weight_y[..., None, :]
    return jnp.einsum('rsaji,rsax->rjsix', weighted, weight_x, precision=highest)

def mesh_forces(windows, atom_data, block_x):
    rows_y, cells_x, atom_count = atom_data.shape[1:]
    corner_x = (jnp.arange(cells_x, dtype=jnp.float32) * block_x)[:, None]
    place_z = atom_data[0].reshape(rows_y, cells_x * atom_count)
    place_y = atom_data[1].reshape(rows_y, cells_x * atom_count)
    place_x = (atom_data[2] + corner_x).reshape(rows_y, cells_x * atom_count)
    charge_rows = atom_data[3].reshape(rows_y, cells_x * atom_count)
    weight_z, slope_z = window_weights(place_z, windows.shape[0])
    weight_y, slope_y = window_weights(place_y, windows.shape[2])
    weight_x, slope_x = periodic_weights(place_x)
    along_x = jnp.einsum('jsix,sax->saji', windows, weight_x, precision=highest)
    across_x = jnp.einsum('jsix,sax->saji', windows, slope_x, precision=highest)
    force_z = -charge_rows * lax.optimization_barrier(jnp.sum(along_x * slope_z[..., :, None] * weight_y[..., None, :], axis=(2, 3)))
    force_y = -charge_rows * lax.optimization_barrier(jnp.sum(along_x * weight_z[..., :, None] * slope_y[..., None, :], axis=(2, 3)))
    force_x = -charge_rows * lax.optimization_barrier(jnp.sum(across_x * weight_z[..., :, None] * weight_y[..., None, :], axis=(2, 3)))
    return jnp.stack([force_z, force_y, force_x])

def influence(wave_z, wave_y, wave_x):

    def frequency(wave_index):
        return jnp.where(wave_index < GRID // 2, wave_index, wave_index - GRID).astype(jnp.float32) / GRID

    def euler_factor(wave_index):
        angles = 2.0 * math.pi / GRID * wave_index.astype(jnp.float32)
        return 1.0 / (2.0 / 3.0 + jnp.cos(angles) / 3.0) ** 2
    wave_square = (2.0 * math.pi) ** 2 * (frequency(wave_z) ** 2 + frequency(wave_y) ** 2 + frequency(wave_x) ** 2)
    safe_square = jnp.where(wave_square > 0.0, wave_square, 1.0)
    volume = float(GRID) ** 3
    value = 4.0 * math.pi / (volume * safe_square) * jnp.exp(-safe_square / (4.0 * ewald_beta ** 2))
    value = value * euler_factor(wave_z) * euler_factor(wave_y) * euler_factor(wave_x)
    return jnp.where(wave_square > 0.0, value, 0.0)

def fold_wrap(values, along, block_size):
    main_part = lax.slice_in_dim(values, 3, block_size + 3, axis=along + 1)
    tail_part = jnp.roll(lax.slice_in_dim(values, 0, 3, axis=along + 1), -1, axis=along)
    widths = [(0, 0)] * values.ndim
    widths[along + 1] = (block_size - 3, 0)
    summed = main_part + jnp.pad(tail_part, widths)
    old_shape = values.shape
    return summed.reshape(old_shape[:along] + (old_shape[along] * block_size,) + old_shape[along + 2:])

def unfold(values, block_count, block_size):
    planes = values.shape[0]
    length = values.shape[2]
    head_part = values[:, :block_count * block_size].reshape(planes, block_count, block_size, length)
    rest_part = jnp.pad(values[:, block_size:], ((0, 0), (0, block_size - 3), (0, 0)))
    rest_part = rest_part.reshape(planes, block_count, block_size, length)[:, :, :3]
    return jnp.concatenate([head_part, rest_part], 2)

def reference(positions, charges, neighbours):
    cell_box = jnp.array([PZ, BY, BX], jnp.float32)
    atom_data = jnp.concatenate([positions * cell_box[:, None, None, None, None], charges[None]], 0)
    flat_cells = atom_data.reshape(4, NCZ * NCY * CX, ATOMS)
    index_y = jnp.arange(NCY, dtype=jnp.int32)[:, None]
    index_x = jnp.arange(CX, dtype=jnp.int32)[None, :]
    row_list = jnp.arange(NCZ, dtype=jnp.int32)

    def short_row(row_z):
        own_cells = lax.dynamic_index_in_dim(atom_data, row_z, 1, keepdims=False).reshape(4, NCY * CX, ATOMS)
        listed = lax.dynamic_index_in_dim(neighbours, row_z, 0, keepdims=False)
        summed = jnp.zeros((3, NCY * CX, ATOMS), jnp.float32)
        for entry_index in range(K):
            stencil = listed[:, :, entry_index]
            step_z = stencil // 9 - 1
            step_y = stencil // 3 % 3 - 1
            step_x = stencil % 3 - 1
            flat_index = (((row_z + step_z) % NCZ * NCY + (index_y + step_y) % NCY) * CX + (index_x + step_x) % CX).reshape(-1)
            other_cells = jnp.take(flat_cells, flat_index, axis=1)
            offset = jnp.stack([step_z * PZ, step_y * BY, step_x * BX]).reshape(3, NCY * CX).astype(jnp.float32)
            summed = summed + pair_terms(own_cells, other_cells, offset)
        return summed
    short_range = lax.map(short_row, row_list)

    def patch_row(row_z):
        row_atoms = lax.dynamic_slice_in_dim(atom_data, row_z, 1, 1)
        return spread_rows(row_atoms, PZ + 3, BY + 3, BX)[0]
    patches = lax.map(patch_row, row_list)
    charge_grid = fold_wrap(fold_wrap(patches, 0, PZ), 1, BY)
    spectrum = jnp.fft.fftn(charge_grid)
    wave_index = jnp.arange(GRID, dtype=jnp.int32)
    kernel = influence(wave_index[:, None, None], wave_index[None, :, None], wave_index[None, None, :])
    potential = jnp.real(jnp.fft.ifftn(spectrum * kernel)) * float(GRID) ** 3
    extended = jnp.concatenate([potential[-3:], potential], 0)
    extended = jnp.concatenate([extended[:, -3:], extended], 1)

    def mesh_row(row_z):
        plane_block = lax.dynamic_slice_in_dim(extended, row_z * PZ, PZ + 3, 0)
        windows = unfold(plane_block, NCY, BY)
        row_atoms = lax.dynamic_index_in_dim(atom_data, row_z, 1, keepdims=False)
        return mesh_forces(windows, row_atoms, BX)
    mesh_part = lax.map(mesh_row, row_list)
    combined = short_range.reshape(NCZ, 3, NCY, CX, ATOMS) + mesh_part.reshape(NCZ, 3, NCY, CX, ATOMS)
    return jnp.transpose(combined, (1, 0, 2, 3, 4))
```

```python
import math

import jax
import jax.numpy as jnp
from jax import lax
from jax.sharding import PartitionSpec as P

GRID = 256


ewald_beta = 0.7
soften = 1.0
highest = lax.Precision.HIGHEST
high = lax.Precision.HIGH


def with_halo(cells, sides, width):
    for axis, dim in sides:
        count = lax.axis_size(axis)
        head = lax.slice_in_dim(cells, 0, width, axis=dim)
        tail = lax.slice_in_dim(cells, cells.shape[dim] - width, cells.shape[dim], axis=dim)
        cells = jnp.concatenate(
            [
                lax.ppermute(tail, axis, [(i, (i + 1) % count) for i in range(count)]),
                cells,
                lax.ppermute(head, axis, [((i + 1) % count, i) for i in range(count)]),
            ],
            axis=dim,
        )
    return cells


def shifted(shard, axis, by):
    count = lax.axis_size(axis)
    return lax.ppermute(shard, axis, [(i, (i + by) % count) for i in range(count)])


def bspline(offsets):
    clipped = jnp.clip(offsets, 0.0, 4.0)
    lift_one = jnp.maximum(clipped - 1.0, 0.0)
    lift_two = jnp.maximum(clipped - 2.0, 0.0)
    lift_three = jnp.maximum(clipped - 3.0, 0.0)
    spline_value = (clipped**3 - 4.0 * lift_one**3 + 6.0 * lift_two**3 - 4.0 * lift_three**3) / 6.0
    spline_slope = (clipped**2 - 4.0 * lift_one**2 + 6.0 * lift_two**2 - 4.0 * lift_three**2) / 2.0
    return (spline_value, spline_slope)


def window_weights(coords, span):
    return bspline(coords[..., None] + 3.0 - jnp.arange(span, dtype=jnp.float32))


def periodic_weights(coords):
    offsets = coords[..., None] - jnp.arange(GRID, dtype=jnp.float32)
    offsets = jnp.where(offsets < 0.0, offsets + GRID, offsets)
    return bspline(offsets)


def pair_terms(own_cells, other_cells, offset):
    displace = own_cells[:3, :, :, None] - other_cells[:3, :, None, :] - offset[:, :, None, None]
    dist_square = jnp.sum(displace * displace, axis=0) + soften
    distance = jnp.sqrt(dist_square)
    scaled = ewald_beta * distance
    radial = (
        jax.scipy.special.erfc(scaled) / distance
        + 2.0 * ewald_beta / math.sqrt(math.pi) * jnp.exp(-scaled * scaled)
    ) / dist_square
    weight = own_cells[3][:, :, None] * other_cells[3][:, None, :] * radial
    return jnp.sum(weight[None] * displace, axis=3)


def spread_rows(atom_data, span_z, span_y, block_x):
    rows_z, rows_y, cells_x, atom_count = atom_data.shape[1:]
    corner_x = (jnp.arange(cells_x, dtype=jnp.float32) * block_x)[:, None]
    place_z = atom_data[0].reshape(rows_z, rows_y, cells_x * atom_count)
    place_y = atom_data[1].reshape(rows_z, rows_y, cells_x * atom_count)
    place_x = (atom_data[2] + corner_x).reshape(rows_z, rows_y, cells_x * atom_count)
    charge_rows = atom_data[3].reshape(rows_z, rows_y, cells_x * atom_count)
    weight_z = window_weights(place_z, span_z)[0]
    weight_y = window_weights(place_y, span_y)[0]
    weight_x = periodic_weights(place_x)[0]
    weighted = charge_rows[..., None, None] * weight_z[..., :, None] * weight_y[..., None, :]
    return jnp.einsum("rsaji,rsax->rjsix", weighted, weight_x, precision=high)


def mesh_forces(windows, atom_data, block_x):
    rows_y, cells_x, atom_count = atom_data.shape[1:]
    corner_x = (jnp.arange(cells_x, dtype=jnp.float32) * block_x)[:, None]
    place_z = atom_data[0].reshape(rows_y, cells_x * atom_count)
    place_y = atom_data[1].reshape(rows_y, cells_x * atom_count)
    place_x = (atom_data[2] + corner_x).reshape(rows_y, cells_x * atom_count)
    charge_rows = atom_data[3].reshape(rows_y, cells_x * atom_count)
    weight_z, slope_z = window_weights(place_z, windows.shape[0])
    weight_y, slope_y = window_weights(place_y, windows.shape[2])
    weight_x, slope_x = periodic_weights(place_x)
    along_x = jnp.einsum("jsix,sax->saji", windows, weight_x, precision=highest)
    across_x = jnp.einsum("jsix,sax->saji", windows, slope_x, precision=highest)
    force_z = -charge_rows * jnp.sum(
        along_x * slope_z[..., :, None] * weight_y[..., None, :], axis=(2, 3)
    )
    force_y = -charge_rows * jnp.sum(
        along_x * weight_z[..., :, None] * slope_y[..., None, :], axis=(2, 3)
    )
    force_x = -charge_rows * jnp.sum(
        across_x * weight_z[..., :, None] * weight_y[..., None, :], axis=(2, 3)
    )
    return jnp.stack([force_z, force_y, force_x])


def influence(wave_z, wave_y, wave_x):

    def frequency(wave_index):
        return (
            jnp.where(wave_index < GRID // 2, wave_index, wave_index - GRID).astype(jnp.float32)
            / GRID
        )

    def euler_factor(wave_index):
        angles = 2.0 * math.pi / GRID * wave_index.astype(jnp.float32)
        return 1.0 / (2.0 / 3.0 + jnp.cos(angles) / 3.0) ** 2

    wave_square = (2.0 * math.pi) ** 2 * (
        frequency(wave_z) ** 2 + frequency(wave_y) ** 2 + frequency(wave_x) ** 2
    )
    safe_square = jnp.where(wave_square > 0.0, wave_square, 1.0)
    volume = float(GRID) ** 3
    value = 4.0 * math.pi / (volume * safe_square) * jnp.exp(-safe_square / (4.0 * ewald_beta**2))
    value = value * euler_factor(wave_z) * euler_factor(wave_y) * euler_factor(wave_x)
    return jnp.where(wave_square > 0.0, value, 0.0)


def dft_table(direction):
    points = jnp.arange(GRID, dtype=jnp.int32)
    product = points[:, None] * points[None, :] % GRID
    angles = 2.0 * math.pi / GRID * product.astype(jnp.float32)
    cosine = jnp.cos(angles)
    sine_part = direction * jnp.sin(angles)
    return jnp.stack([jnp.stack([cosine, sine_part], 1), jnp.stack([-sine_part, cosine], 1)], 0)


def alternating():
    points = jnp.arange(GRID, dtype=jnp.int32)
    return jnp.where(points % 2 == 0, 1.0, -1.0).astype(jnp.float32)


def half_forward():
    points = jnp.arange(GRID, dtype=jnp.int32)
    wave_list = points[: GRID // 2]
    product = points[:, None] * wave_list[None, :] % GRID
    angles = 2.0 * math.pi / GRID * product.astype(jnp.float32)
    real_part = jnp.cos(angles)
    imag_part = jnp.where(wave_list[None, :] == 0, alternating()[:, None], -jnp.sin(angles))
    return jnp.stack([real_part, imag_part], 1)


def half_inverse():
    points = jnp.arange(GRID, dtype=jnp.int32)
    wave_list = points[: GRID // 2]
    product = wave_list[:, None] * points[None, :] % GRID
    angles = 2.0 * math.pi / GRID * product.astype(jnp.float32)
    real_part = jnp.where(wave_list[:, None] == 0, 1.0, 2.0 * jnp.cos(angles))
    imag_part = jnp.where(wave_list[:, None] == 0, alternating()[None, :], -2.0 * jnp.sin(angles))
    return jnp.stack([real_part, imag_part], 0)


def packed_forward():
    points = jnp.arange(GRID, dtype=jnp.int32)
    product = points[:, None] * points[None, :] % GRID
    angles = 2.0 * math.pi / GRID * product.astype(jnp.float32)
    cosine = jnp.cos(angles)
    sine = jnp.sin(angles)
    wave_list = points[None, :]
    low_band = (wave_list > 0) & (wave_list < GRID // 2)
    high_band = wave_list > GRID // 2
    at_edge = (wave_list == 0) | (wave_list == GRID // 2)
    blank = jnp.zeros_like(cosine)
    real_keep = jnp.where(low_band | at_edge, cosine, blank)
    real_turn = jnp.where(low_band, -sine, blank)
    imag_turn = jnp.where(high_band, cosine, blank)
    imag_keep = jnp.where(high_band, sine, jnp.where(at_edge, cosine, blank))
    return jnp.stack(
        [jnp.stack([real_keep, real_turn], 1), jnp.stack([imag_turn, imag_keep], 1)], 0
    )


def packed_inverse():
    points = jnp.arange(GRID, dtype=jnp.int32)
    product = points[:, None] * points[None, :] % GRID
    angles = 2.0 * math.pi / GRID * product.astype(jnp.float32)
    cosine = jnp.cos(angles)
    sine = jnp.sin(angles)
    wave_list = points[:, None]
    low_band = (wave_list > 0) & (wave_list < GRID // 2)
    high_band = wave_list > GRID // 2
    at_edge = (wave_list == 0) | (wave_list == GRID // 2)
    blank = jnp.zeros_like(cosine)
    real_keep = jnp.where(at_edge, cosine, jnp.where(low_band, 2.0 * cosine, blank))
    real_turn = jnp.where(high_band, 2.0 * cosine, blank)
    imag_turn = jnp.where(low_band, -2.0 * sine, blank)
    imag_keep = jnp.where(at_edge, cosine, jnp.where(high_band, 2.0 * sine, blank))
    return jnp.stack(
        [jnp.stack([real_keep, real_turn], 1), jnp.stack([imag_turn, imag_keep], 1)], 0
    )


def packed_kernel(column, zero_kernel, half_kernel, packed_wave, mirror_axis):
    at_edge = (packed_wave == 0) | (packed_wave == GRID // 2)
    low_band = packed_wave < GRID // 2
    direct = jnp.where(
        at_edge, 0.5 * (zero_kernel + half_kernel), jnp.where(low_band, zero_kernel, half_kernel)
    )
    crossed = jnp.where(at_edge, 0.5 * (zero_kernel - half_kernel), 0.0)
    mirrored = jnp.roll(jnp.flip(column, mirror_axis), 1, mirror_axis)
    conjugate = jnp.stack([mirrored[0], -mirrored[1]])
    return direct[None] * column + crossed[None] * conjugate


def fold_rows(values, along, block_size):
    rows = values.shape[along]
    main_part = lax.slice_in_dim(
        lax.slice_in_dim(values, 0, rows - 1, axis=along), 3, block_size + 3, axis=along + 1
    )
    tail_part = lax.slice_in_dim(
        lax.slice_in_dim(values, 1, rows, axis=along), 0, 3, axis=along + 1
    )
    widths = [(0, 0)] * values.ndim
    widths[along + 1] = (block_size - 3, 0)
    summed = main_part + jnp.pad(tail_part, widths)
    old_shape = values.shape
    return summed.reshape(old_shape[:along] + ((rows - 1) * block_size,) + old_shape[along + 2 :])


def unfold(values, block_count, block_size):
    planes = values.shape[0]
    length = values.shape[2]
    head_part = values[:, : block_count * block_size].reshape(
        planes, block_count, block_size, length
    )
    rest_part = jnp.pad(values[:, block_size:], ((0, 0), (0, block_size - 3), (0, 0)))
    rest_part = rest_part.reshape(planes, block_count, block_size, length)[:, :, :3]
    return jnp.concatenate([head_part, rest_part], 2)


def over_ranks(values):
    return lax.all_to_all(values, ("rank", "sub"), split_axis=0, concat_axis=0, tiled=True)


def over_domains(values):
    return lax.all_to_all(values, "dom", split_axis=0, concat_axis=0, tiled=True)


def matmul(left, right, precision):
    return jnp.dot(left, right, precision=precision)


def replace_first(values, first, count):
    holder = lax.axis_index(("rank", "sub")) == 0
    kept = lax.slice_in_dim(values, 0, count, axis=values.ndim - 1)
    return lax.dynamic_update_slice_in_dim(
        values, jnp.where(holder, first, kept), 0, axis=values.ndim - 1
    )


def ranks_first_half(charge_grid, domain_count, rank_count):
    plane_count = charge_grid.shape[0]
    row_count = charge_grid.shape[1]
    kx_count = GRID // 2 // rank_count
    ky_count = GRID // domain_count
    forward = dft_table(-1.0)
    inverse = dft_table(1.0)
    wave_x = lax.axis_index(("rank", "sub")) * kx_count + jnp.arange(kx_count, dtype=jnp.int32)

    def forward_y(table):
        table = table.reshape(2, rank_count, row_count, 2, domain_count, ky_count)
        return table.transpose(4, 3, 5, 1, 0, 2).reshape(2 * GRID, 2 * GRID)

    def inverse_y(table):
        table = table.reshape(2, domain_count, ky_count, 2, rank_count, row_count)
        return table.transpose(4, 3, 5, 1, 0, 2).reshape(2 * GRID, 2 * GRID)

    spectrum = jnp.einsum(
        "zyx,xcdk->dcykz",
        charge_grid,
        half_forward().reshape(GRID, 2, rank_count, kx_count),
        precision=high,
    ).reshape(rank_count, 2 * row_count, kx_count * plane_count)
    arrived = over_ranks(spectrum).reshape(2 * GRID, kx_count * plane_count)
    spectrum = matmul(forward_y(forward), arrived, high)
    packed = matmul(forward_y(packed_forward()), arrived[:, :plane_count], high)
    spectrum = replace_first(spectrum, packed, plane_count)
    arrived = over_domains(spectrum.reshape(domain_count, 2 * ky_count, kx_count * plane_count))
    arrived = arrived.reshape(domain_count, 2, ky_count, kx_count, plane_count)
    arrived = arrived.transpose(0, 1, 4, 3, 2).reshape(2 * GRID, kx_count * ky_count)
    forward_z = forward.reshape(2, domain_count, plane_count, 2, GRID)
    forward_z = forward_z.transpose(3, 4, 1, 0, 2).reshape(2 * GRID, 2 * GRID)
    spectrum = matmul(forward_z, arrived, high).reshape(2, GRID, kx_count * ky_count)
    plane_wave = jnp.arange(GRID, dtype=jnp.int32)[:, None]
    row_line = lax.axis_index("dom") * ky_count + jnp.arange(ky_count, dtype=jnp.int32)
    row_wave = row_line[None, :]
    scaled = (
        spectrum
        * influence(
            plane_wave, jnp.tile(row_line, kx_count)[None, :], jnp.repeat(wave_x, ky_count)[None, :]
        )[None]
    )
    zero_kernel = influence(plane_wave, row_wave, jnp.zeros_like(row_wave))
    half_kernel = influence(plane_wave, row_wave, jnp.full_like(row_wave, GRID // 2))
    packed = packed_kernel(spectrum[..., :ky_count], zero_kernel, half_kernel, row_wave, 1)
    spectrum = replace_first(scaled, packed, ky_count).reshape(2 * GRID, kx_count * ky_count)
    inverse_z = inverse.reshape(2, GRID, 2, domain_count, plane_count)
    inverse_z = inverse_z.transpose(3, 2, 4, 0, 1).reshape(2 * GRID, 2 * GRID)
    returned = matmul(inverse_z, spectrum, highest)
    arrived = over_domains(returned.reshape(domain_count, 2 * plane_count, kx_count * ky_count))
    arrived = arrived.reshape(domain_count, 2, plane_count, kx_count, ky_count)
    arrived = arrived.transpose(0, 1, 4, 3, 2).reshape(2 * GRID, kx_count * plane_count)
    returned = matmul(inverse_y(inverse), arrived, highest)
    packed = matmul(inverse_y(packed_inverse()), arrived[:, :plane_count], highest)
    returned = replace_first(returned, packed, plane_count)
    arrived = over_ranks(returned.reshape(rank_count, 2 * row_count, kx_count * plane_count))
    return jnp.einsum(
        "scykz,cskx->zyx",
        arrived.reshape(rank_count, 2, row_count, kx_count, plane_count),
        half_inverse().reshape(2, rank_count, kx_count, GRID),
        precision=highest,
    )


def local(positions, charges, neighbours):
    domain_count = lax.axis_size("dom")
    rank_count = lax.axis_size(("rank", "sub"))
    plane_count = GRID // domain_count
    row_count = GRID // rank_count
    cells_y = positions.shape[2]
    cells_x = positions.shape[3]
    atom_count = positions.shape[4]
    block_y = row_count // cells_y
    block_x = GRID // cells_x
    cell_box = jnp.array([plane_count, block_y, block_x], jnp.float32)
    packed = jnp.concatenate([positions * cell_box[:, None, None, None, None], charges[None]], 0)
    padded = with_halo(packed, (("dom", 1), (("rank", "sub"), 2)), 1)
    cell_count = cells_y * cells_x
    own_cells = padded[:, 1, 1 : cells_y + 1].reshape(4, cell_count, atom_count)
    flat_cells = padded.reshape(4, 3 * (cells_y + 2) * cells_x, atom_count)
    index_y = jnp.arange(cells_y, dtype=jnp.int32)[:, None]
    index_x = jnp.arange(cells_x, dtype=jnp.int32)[None, :]
    short_range = jnp.zeros((3, cell_count, atom_count), jnp.float32)
    for entry_index in range(neighbours.shape[3]):
        stencil = neighbours[0, :, :, entry_index]
        step_z = stencil // 9 - 1
        step_y = stencil // 3 % 3 - 1
        step_x = stencil % 3 - 1
        flat_index = (
            ((1 + step_z) * (cells_y + 2) + index_y + 1 + step_y) * cells_x
            + (index_x + step_x) % cells_x
        ).reshape(-1)
        other_cells = jnp.take(flat_cells, flat_index, axis=1)
        offset = (
            jnp.stack([step_z * plane_count, step_y * block_y, step_x * block_x])
            .reshape(3, cell_count)
            .astype(jnp.float32)
        )
        short_range = short_range + pair_terms(own_cells, other_cells, offset)
    patches = spread_rows(padded[:, 1:3, 1 : cells_y + 2], plane_count + 3, block_y + 3, block_x)
    charge_grid = fold_rows(fold_rows(patches, 0, plane_count), 1, block_y)
    potential = ranks_first_half(charge_grid, domain_count, rank_count)
    below = shifted(potential[plane_count - 3 :], "dom", 1)
    extended = jnp.concatenate([below, potential], 0)
    beside = shifted(extended[:, row_count - 3 :], ("rank", "sub"), 1)
    extended = jnp.concatenate([beside, extended], 1)
    windows = unfold(extended, cells_y, block_y)
    mesh_part = mesh_forces(windows, padded[:, 1, 1 : cells_y + 1], block_x)
    combined = short_range.reshape(3, cells_y, cells_x, atom_count) + mesh_part.reshape(
        3, cells_y, cells_x, atom_count
    )
    return combined[:, None]


def solution(mesh):
    return jax.shard_map(
        local,
        mesh=mesh,
        in_specs=(
            P(None, ("sys", "dom"), ("rank", "sub"), None, None),
            P(("sys", "dom"), ("rank", "sub"), None, None),
            P(("sys", "dom"), ("rank", "sub"), None, None),
        ),
        out_specs=P(None, ("sys", "dom"), ("rank", "sub"), None, None),
        check_vma=False,
    )
```
